128 devices in a mesh: replica: 32 (over y, x, z_hi), tensor: 4 (over z_lo, core).
Axes of the slice: x: 4, y: 4, z: 4 (z_hi: 2, z_lo: 2; z = z_hi * 2 + z_lo), core: 2. Of those that a mesh axis runs over, the one named last changes fastest.
Arguments:
- weights: bfloat16 [32, 7168, 2048], P('replica', 'tensor'), may hold values from -6 to 6
- hidden: bfloat16 [32, 2, 512, 7168], P('replica', None, None, 'tensor'), may hold values from -6 to 6
- targets: bfloat16 [32, 2, 512, 2048], P('replica'), may hold values from -6 to 6
- norm_gain: float32 [2048], replicated, may hold values from 0.5 to 2
- stragglers: int32 [2, 32], replicated, may hold values 0 or 1
Outputs:
- new_weights: bfloat16 [32, 7168, 2048], P('replica', 'tensor')
The draws below stay inside these ranges and needn't reach their ends.
All inputs are finite; a program needn't handle non-finite values.
Results may differ from the reference program's by a relative error of at most 0.011.
Values may be sent and summed in bfloat16 or wider, within the bound.
No kernel may reach another device: no remote copies, remote signals or barrier semaphores. Data moves between devices by JAX's collectives and lax.ppermute only.
A program may use at most 128 MiB of HBM per device.

```python
import math
import jax
import jax.numpy as jnp
from jax import lax

D = 2048
FF = 7168
TOK_DEV = 512
STEPS = 2
REPLICAS = 32
N_REPLICA = 32


def set_ends(entries, own_key, low, high):
    place = [jax.random.randint(jax.random.fold_in(own_key, axis), (), 0, length) for axis, length in enumerate(entries.shape)]
    widest = entries.shape.index(max(entries.shape))
    neighbour = place[:widest] + [(place[widest] + 1) % entries.shape[widest]] + place[widest + 1:]
    return entries.at[tuple(place)].set(low).at[tuple(neighbour)].set(high)


def block_levels(key, dims, shards, smallest, top_value):
    loudness, own = 1.0, jax.random.fold_in(key, 6)
    for position, blocks in shards:
        heights = jnp.exp(jax.random.uniform(jax.random.fold_in(own, position), (blocks,), jnp.float32, smallest / len(shards), top_value / len(shards)))
        loudness = loudness * jnp.repeat(heights, dims[position] // blocks).reshape([-1 if axis == position else 1 for axis in range(len(dims))])
    return loudness


def centred(rng, dims, spread, most, shards=(), held_as=jnp.bfloat16):
    factor_of = block_levels(rng, dims, shards, -0.22, 0.18) if shards else 1.0
    drawn = jax.random.normal(rng, dims, jnp.float32) * spread * factor_of
    return jnp.minimum(jnp.maximum(drawn, -most), most).astype(held_as)


def setup_inputs(seed: int = 0) -> dict:
    arg_keys = jax.random.split(jax.random.key(seed), 6)
    return {
        "weights": centred(arg_keys[0], (REPLICAS, FF, D), 1.0, 6.0, ((0, 32), (1, 4))),
        "hidden": centred(arg_keys[1], (REPLICAS, STEPS, TOK_DEV, FF), 1.0, 6.0, ((0, 32), (3, 4))),
        "targets": centred(arg_keys[2], (REPLICAS, STEPS, TOK_DEV, D), 1.0, 6.0, ((0, 32),)),
        "norm_gain": jnp.clip(jnp.exp(jax.random.uniform(arg_keys[3], (D,), jnp.float32, math.log(0.5), math.log(2.0))), 0.5, 2.0),
        "stragglers": set_ends((jax.random.randint(arg_keys[4], (STEPS, REPLICAS), 0, 4) < 1).astype(jnp.int32), jax.random.fold_in(arg_keys[4], 1), 0, 1),
    }


eps = 1e-05
learn_rate = 0.5

def contract_rows(left, right):
    return lax.dot_general(left, right, (((0,), (0,)), ((), ())), preferred_element_type=jnp.float32)

def norm_backward(outputs, target_rows, norm_gain):
    squares = lax.optimization_barrier(jnp.mean(outputs * outputs, axis=-1, keepdims=True))
    inverse = lax.rsqrt(squares + eps)
    normed = outputs * inverse
    weighted = (normed * norm_gain - target_rows.astype(jnp.float32)) * norm_gain
    cross_mean = lax.optimization_barrier(jnp.mean(weighted * normed, axis=-1, keepdims=True))
    return (inverse * (weighted - normed * cross_mean)).astype(jnp.bfloat16)

def local_update(weight_block, hidden_rows, target_rows, norm_gain):
    factor = FF ** (-0.5)
    outputs = factor * jnp.dot(hidden_rows, weight_block, preferred_element_type=jnp.float32)
    grad_out = norm_backward(outputs, target_rows, norm_gain)
    grad_weight = (factor * contract_rows(hidden_rows, grad_out)).astype(jnp.bfloat16)
    return (weight_block.astype(jnp.float32) - learn_rate * grad_weight.astype(jnp.float32)).astype(jnp.bfloat16)

def reference(weights, hidden, targets, norm_gain, stragglers):
    levels = N_REPLICA.bit_length() - 1
    indices = jnp.arange(N_REPLICA, dtype=jnp.int32)
    for update_step in range(STEPS):
        bit_index = update_step % levels
        updated = lax.map(lambda element: local_update(element[0], element[1], element[2], norm_gain), (weights, hidden[:, update_step], targets[:, update_step]))
        partner = jnp.bitwise_xor(indices, jnp.int32(1 << bit_index)).astype(jnp.int32)
        paired = updated[partner]
        mask_row = stragglers[update_step]
        keep_pair = (mask_row == 0) & (mask_row[partner] == 0)
        averaged = ((updated.astype(jnp.float32) + paired.astype(jnp.float32)) * 0.5).astype(jnp.bfloat16)
        weights = jnp.where(keep_pair[:, None, None], averaged, updated)
    return weights
```

```python
import jax
import jax.numpy as jnp
from jax import lax
from jax.experimental import pallas as pl
from jax.experimental.pallas import tpu as pltpu
from jax.sharding import PartitionSpec as P

FF = 7168
EPS = 1e-05
LEARN_RATE = 0.5
FACTOR = FF ** (-0.5)
CHUNKS = 7
GROUPS = tuple((i, 1) for i in range(CHUNKS))


def mm(left, right):
    return jnp.dot(left, right, preferred_element_type=jnp.float32)


def mm_rows(left, right):
    return lax.dot_general(left, right, (((0,), (0,)), ((), ())), preferred_element_type=jnp.float32)


def meet(*values):
    return lax.optimization_barrier(values)


def call(body, grid, in_specs, out_specs, out_shape, name, vmem_mib, aliases=None, scratch=()):
    return pl.pallas_call(
        body,
        grid_spec=pltpu.PrefetchScalarGridSpec(
            num_scalar_prefetch=2,
            grid=grid,
            in_specs=in_specs,
            out_specs=out_specs,
            scratch_shapes=list(scratch),
        ),
        out_shape=out_shape,
        input_output_aliases=aliases or {},
        compiler_params=pltpu.CompilerParams(vmem_limit_bytes=vmem_mib * 1024 * 1024),
        cost_estimate=pl.CostEstimate(flops=1, bytes_accessed=1, transcendentals=0),
        name=name,
    )


def on_device(weights, hidden, targets, norm_gain, stragglers):
    replicas, shards = lax.axis_size("replica"), lax.axis_size("tensor")
    tokens, ff = hidden.shape[2], hidden.shape[3]
    features = weights.shape[2]
    half = tokens // 2
    wide = features // 2
    cols = features // 4
    rows = ff // CHUNKS
    deep = ff // 2
    replica = lax.axis_index("replica")
    core = lax.rem(lax.axis_index("tensor"), 2)
    gain = norm_gain.reshape(1, features)
    raw_hidden = hidden
    weights, hidden, targets = (pltpu.with_memory_space_constraint(a, pltpu.HBM) for a in (weights, hidden, targets))
    place = jnp.stack([core, 1 - core]).astype(jnp.int32)
    turn = [place]

    def permute(block, flip_replica, flip_tensor):
        route = [
            (r * shards + t, (r ^ flip_replica) * shards + (t ^ flip_tensor))
            for r in range(replicas)
            for t in range(shards)
        ]
        return lax.ppermute(block, ("replica", "tensor"), route)

    def run(kernel, *args):
        out = kernel(turn[0], *args)
        several = isinstance(out, (list, tuple))
        turn[0], *out = meet(turn[0], *(out if several else [out]))
        return out if several else out[0]

    def grid_block(shape):
        return pl.BlockSpec(shape, lambda n, p, c: (0, n))

    def term_block(index):
        return pl.BlockSpec((rows, cols), lambda n, p, c: (index, n))

    def pair_shapes():
        return [
            jax.ShapeDtypeStruct((half, wide), jnp.bfloat16),
            jax.ShapeDtypeStruct((half, wide), jnp.float32),
        ]

    def split_store(p, total, send, keep, acc):
        acc[...] = total
        keep[...] = acc[pl.ds(pl.multiple_of(p[0] * half, half), half), :]
        send[...] = acc[pl.ds(pl.multiple_of(p[1] * half, half), half), :].astype(send.dtype)

    split_out = [grid_block((half, cols)), grid_block((half, cols))]
    split_scratch = [pltpu.VMEM((tokens, cols), jnp.float32)]

    def forward(side):
        def body(p, c, h, *refs):
            *w, send, keep, acc = refs
            total = sum(mm(h[0, 0, :, i * deep : (i + 1) * deep], w[i][0]) for i in range(2))
            split_store(p, FACTOR * total, send, keep, acc)

        def weight_block(i):
            return pl.BlockSpec((1, deep, cols), lambda n, p, c: (0, i, 2 * side + n))

        return run(
            call(
                body,
                (2,),
                [pl.BlockSpec((1, 1, tokens, ff), lambda n, p, c: (0, 0, 0, 0))]
                + [weight_block(i) for i in range(2)],
                split_out,
                pair_shapes(),
                "forward",
                20,
                scratch=split_scratch,
            ),
            place,
            hidden,
            *[weights] * 2,
        )

    def norm_backward(step, summed, received):
        tile = half // 2
        strip = min(16, tile)

        def body(p, c, s0, s1, r0, r1, t, g, o):
            for i in range(tile // strip):
                span = slice(i * strip, (i + 1) * strip)
                left = s0[span, :].astype(jnp.float32) + r0[span, :].astype(jnp.float32)
                right = s1[span, :].astype(jnp.float32) + r1[span, :].astype(jnp.float32)
                outputs = jnp.concatenate([left, right], axis=1)
                inverse = lax.rsqrt(jnp.mean(outputs * outputs, axis=-1, keepdims=True) + EPS)
                normed = outputs * inverse
                weighted = (normed * g[...] - t[0, 0, span, :].astype(jnp.float32)) * g[...]
                cross = jnp.mean(weighted * normed, axis=-1, keepdims=True)
                o[span, :] = (inverse * (weighted - normed * cross)).astype(o.dtype)

        side = pl.BlockSpec((tile, wide), lambda i, p, c: (i, 0))
        return run(
            call(
                body,
                (2,),
                [side] * 4
                + [
                    pl.BlockSpec((1, 1, tile, features), lambda i, p, c: (0, step, p[0] * 2 + i, 0)),
                    pl.BlockSpec((1, features), lambda i, p, c: (0, 0)),
                ],
                pl.BlockSpec((tile, features), lambda i, p, c: (i, 0)),
                jax.ShapeDtypeStruct((half, features), jnp.bfloat16),
                "norm_backward",
                16,
            ),
            place,
            *summed,
            *received,
            targets,
            gain,
        )

    def update(groups, grad_own, grad_other):
        total = len(groups)

        def body(p, c, *refs):
            go, gx = refs[:2]
            for i in range(total):
                ho, hx, w, o = (refs[2 + j * total + i] for j in range(4))
                grad = mm_rows(ho[0, 0], go[...]) + mm_rows(hx[0, 0], gx[...])
                grad = (FACTOR * grad).astype(jnp.bfloat16).astype(jnp.float32)
                o[...] = (w[0].astype(jnp.float32) - LEARN_RATE * grad).astype(o.dtype)

        def hidden_block(side, at, count):
            return pl.BlockSpec((1, 1, half, count * rows), lambda n, p, c: (0, 0, p[side], at // count))

        def weight_block(at, count):
            return pl.BlockSpec((1, count * rows, cols), lambda n, p, c: (0, at // count, n))

        return run(
            call(
                body,
                (4,),
                [grid_block((half, cols))] * 2
                + [hidden_block(0, *group) for group in groups]
                + [hidden_block(1, *group) for group in groups]
                + [weight_block(*group) for group in groups],
                [grid_block((count * rows, cols)) for _, count in groups],
                [jax.ShapeDtypeStruct((count * rows, features), jnp.bfloat16) for _, count in groups],
                "update",
                24,
            ),
            place,
            grad_own,
            grad_other,
            *[hidden] * (2 * total),
            *[weights] * total,
        )

    def begin(blocks):
        def body(p, c, h, *refs):
            *w, o = refs
            o[...] = sum(
                mm(h[0, 0, :, at * rows : (at + count) * rows], block[...])
                for (at, count), block in zip(GROUPS, w)
            )

        return run(
            call(
                body,
                (4,),
                [pl.BlockSpec((1, 1, tokens, ff), lambda n, p, c: (0, 1, 0, 0))]
                + [grid_block((count * rows, cols)) for _, count in GROUPS[:-1]],
                grid_block((tokens, cols)),
                jax.ShapeDtypeStruct((tokens, features), jnp.float32),
                "begin",
                20,
            ),
            place,
            hidden,
            *blocks,
        )

    def finish(side, begun, block):
        def body(p, c, a, h, w, send, keep, acc):
            split_store(p, FACTOR * (a[...] + mm(h[0, 0], w[...])), send, keep, acc)

        return run(
            call(
                body,
                (2,),
                [
                    pl.BlockSpec((tokens, cols), lambda n, p, c: (0, 2 * side + n)),
                    pl.BlockSpec((1, 1, tokens, rows), lambda n, p, c: (0, 1, 0, CHUNKS - 1)),
                    pl.BlockSpec((rows, cols), lambda n, p, c: (0, 2 * side + n)),
                ],
                split_out,
                pair_shapes(),
                "finish",
                12,
                scratch=split_scratch,
            ),
            place,
            begun,
            hidden,
            block,
        )

    def output_own(grads, own, got):
        def body(p, c, ho, hx, go, gx, *refs):
            o = refs[-1]
            keep = c[0].astype(jnp.bfloat16)
            gos, gxs = go[...] * keep, gx[...] * keep
            for i, (at, count) in enumerate(GROUPS):
                for k in range(count):
                    span = slice((at + k) * rows, (at + k + 1) * rows)
                    part = slice(k * rows, (k + 1) * rows)
                    grad = mm_rows(ho[0, 0, :, span], gos) + mm_rows(hx[0, 0, :, span], gxs)
                    base = c[0] * refs[i][part, :].astype(jnp.float32)
                    base = base + c[1] * refs[len(GROUPS) + i][part, :].astype(jnp.float32)
                    o[0, span, :] = (base - LEARN_RATE * FACTOR * grad).astype(o.dtype)

        blocks = [grid_block((count * rows, cols)) for _, count in GROUPS]
        return run(
            call(
                body,
                (4,),
                [
                    pl.BlockSpec((1, 1, half, ff), lambda n, p, c: (0, 1, p[0], 0)),
                    pl.BlockSpec((1, 1, half, ff), lambda n, p, c: (0, 1, p[1], 0)),
                ]
                + [grid_block((half, cols))] * 2
                + blocks * 2,
                pl.BlockSpec((1, ff, cols), lambda n, p, c: (0, 0, n)),
                jax.ShapeDtypeStruct(weights.shape, weights.dtype),
                "output_own",
                32,
            ),
            coef,
            hidden,
            hidden,
            *grads,
            *own,
            *got,
        )

    def output_far(grads, base):
        def body(p, c, ho, hx, go, gx, b, o):
            take = c[1].astype(jnp.bfloat16)
            gos, gxs = go[...] * take, gx[...] * take
            for i in range(CHUNKS):
                span = slice(i * rows, (i + 1) * rows)
                grad = mm_rows(ho[:, span], gos) + mm_rows(hx[:, span], gxs)
                total = b[0, span, :].astype(jnp.float32) - LEARN_RATE * FACTOR * grad
                o[0, span, :] = total.astype(o.dtype)

        whole = pl.BlockSpec((1, ff, cols), lambda n, p, c: (0, 0, n))
        return run(
            call(
                body,
                (4,),
                [
                    pl.BlockSpec((half, ff), lambda n, p, c: (p[0], 0)),
                    pl.BlockSpec((half, ff), lambda n, p, c: (p[1], 0)),
                ]
                + [grid_block((half, cols))] * 2
                + [whole],
                whole,
                jax.ShapeDtypeStruct(weights.shape, weights.dtype),
                "output_far",
                28,
            ),
            coef,
            borrowed,
            borrowed,
            *grads,
            base,
        )

    def mix(scale_a, a, scale_b, b):
        return (scale_a * a.astype(jnp.float32) + scale_b * b.astype(jnp.float32)).astype(jnp.bfloat16)

    def add(kept, *parts):
        return sum([part.astype(jnp.float32) for part in parts], kept).astype(jnp.bfloat16)

    sent, kept = zip(*[forward(side) for side in range(2)])
    from_core = [permute(block, 0, 1) for block in sent]
    summed = [add(k, f) for k, f in zip(kept, from_core)]
    summed[0], raw_hidden, late = meet(summed[0], raw_hidden, stragglers)
    lone = raw_hidden[0, 1]
    summed[1], lone = meet(summed[1], lone)
    from_z = [permute(block, 0, 2) for block in summed]
    borrowed = permute(lone, 2, 0)

    def pair(step, low, high):
        count = lax.dynamic_index_in_dim(late[step], low, keepdims=False)
        count += lax.dynamic_index_in_dim(late[step], high, keepdims=False)
        return jnp.where(count == 0, jnp.float32(0.5), jnp.float32(0.0))

    near, mine = pair(0, replica, replica ^ 1), pair(1, replica, replica ^ 2)
    coef = jnp.stack([1 - mine, mine])
    from_z[0], near, coef = meet(from_z[0], near, coef)

    grad_own = norm_backward(0, summed, from_z)
    grad_other = permute(grad_own, 0, 1)

    updated = update(GROUPS[:1], grad_own, grad_other)
    updated += update(GROUPS[1:], grad_own, grad_other)
    got = [permute(block, 1, 0) for block in updated]
    averaged, x_got = [], []
    for i in range(len(GROUPS)):
        if i > 1:
            got[i], x_got[i - 2] = meet(got[i], x_got[i - 2])
        elif i == 0:
            got[i], borrowed = meet(got[i], borrowed)
        averaged.append(mix(1 - near, updated[i], near, got[i]))
        x_got.append(permute(averaged[i], 2, 0))

    begun = begin(averaged[:-1])
    sent, kept = zip(*[finish(side, begun, averaged[-1]) for side in range(2)])
    from_core = [permute(block, 0, 1) for block in sent]
    summed = [add(k, f) for k, f in zip(kept, from_core)]
    summed[1], x_got[-2] = meet(summed[1], x_got[-2])
    from_z = [permute(block, 0, 2) for block in summed]
    *from_z, x_got[-1] = meet(*from_z, x_got[-1])
    next_own = norm_backward(1, summed, from_z)
    next_other = permute(next_own, 0, 1)
    far_own = permute(next_own, 2, 0)
    base = output_own((next_own, next_other), averaged, x_got)
    base = pltpu.with_memory_space_constraint(base, pltpu.HBM)
    base, far_own = meet(base, far_own)
    far_other = permute(far_own, 0, 1)
    return output_far((far_own, far_other), base)


def solution(mesh):
    placed = (
        P("replica", "tensor", None),
        P("replica", None, None, "tensor"),
        P("replica", None, None, None),
        P(),
        P(),
    )
    return jax.shard_map(
        on_device,
        mesh=mesh,
        in_specs=placed,
        out_specs=P("replica", "tensor", None),
        check_vma=False,
    )
```

```python
import jax
import jax.numpy as jnp
from jax import lax
from jax.experimental import pallas as pl
from jax.experimental.pallas import tpu as pltpu
from jax.sharding import PartitionSpec as P

FF = 7168
EPS = 1e-05
LEARN_RATE = 0.5
FACTOR = FF ** (-0.5)
UNITS = 14
GROUPS = tuple((2 * i, 2) for i in range(7))


def mm(left, right):
    return jnp.dot(left, right, preferred_element_type=jnp.float32)


def mm_rows(left, right):
    return lax.dot_general(left, right, (((0,), (0,)), ((), ())), preferred_element_type=jnp.float32)


def meet(*values):
    return lax.optimization_barrier(values)


def call(body, grid, in_specs, out_specs, out_shape, name, vmem_mib, aliases=None, scratch=()):
    return pl.pallas_call(
        body,
        grid_spec=pltpu.PrefetchScalarGridSpec(
            num_scalar_prefetch=2,
            grid=grid,
            in_specs=in_specs,
            out_specs=out_specs,
            scratch_shapes=list(scratch),
        ),
        out_shape=out_shape,
        input_output_aliases=aliases or {},
        compiler_params=pltpu.CompilerParams(vmem_limit_bytes=vmem_mib * 1024 * 1024),
        cost_estimate=pl.CostEstimate(flops=1, bytes_accessed=1, transcendentals=0),
        name=name,
    )


def on_device(weights, hidden, targets, norm_gain, stragglers):
    replicas, shards = lax.axis_size("replica"), lax.axis_size("tensor")
    tokens, ff = hidden.shape[2], hidden.shape[3]
    features = weights.shape[2]
    half = tokens // 2
    cols = features // 4
    narrow = features // 8
    unit = ff // UNITS
    deep = ff // 2
    edge = 8 * unit
    replica = lax.axis_index("replica")
    core = lax.rem(lax.axis_index("tensor"), 2)
    near_z = lax.div(lax.axis_index("tensor"), 2)
    quarter = tokens // 4
    gain = norm_gain.reshape(1, features)
    raw_hidden = hidden
    weights, hidden, targets = (pltpu.with_memory_space_constraint(a, pltpu.HBM) for a in (weights, hidden, targets))
    place = jnp.stack([core, 1 - core, near_z, 1 - near_z]).astype(jnp.int32)
    turn = [place]

    def permute(block, flip_replica, flip_tensor):
        route = [
            (r * shards + t, (r ^ flip_replica) * shards + (t ^ flip_tensor))
            for r in range(replicas)
            for t in range(shards)
        ]
        return lax.ppermute(block, ("replica", "tensor"), route)

    def run(kernel, *args):
        out = kernel(turn[0], *args)
        several = isinstance(out, (list, tuple))
        turn[0], *out = meet(turn[0], *(out if several else [out]))
        return out if several else out[0]

    def grid_block(shape):
        return pl.BlockSpec(shape, lambda n, p, c: (0, n))

    def forward():
        def body(p, c, h, w0, w1, send, keep, acc):
            total = mm(h[0, 0, :, :deep], w0[0]) + mm(h[0, 0, :, deep:], w1[0])
            acc[...] = FACTOR * total
            keep[...] = acc[pl.ds(pl.multiple_of(p[0] * half, half), half), :]
            send[...] = acc[pl.ds(pl.multiple_of(p[1] * half, half), half), :].astype(send.dtype)

        return run(
            call(
                body,
                (4,),
                [
                    pl.BlockSpec((1, 1, tokens, ff), lambda n, p, c: (0, 0, 0, 0)),
                    pl.BlockSpec((1, deep, cols), lambda n, p, c: (0, 0, n)),
                    pl.BlockSpec((1, deep, cols), lambda n, p, c: (0, 1, n)),
                ],
                [grid_block((half, cols))] * 2,
                [
                    jax.ShapeDtypeStruct((half, features), jnp.bfloat16),
                    jax.ShapeDtypeStruct((half, features), jnp.float32),
                ],
                "forward",
                14,
                scratch=[pltpu.VMEM((tokens, cols), jnp.float32)],
            ),
            place,
            hidden,
            weights,
            weights,
        )

    def norm_backward(step, summed, received):
        size = summed.shape[0]
        tile = size // 2
        strip = min(16, tile)

        def body(p, c, s, r, t, g, o):
            for i in range(tile // strip):
                span = slice(i * strip, (i + 1) * strip)
                outputs = s[span, :].astype(jnp.float32) + r[span, :].astype(jnp.float32)
                inverse = lax.rsqrt(jnp.mean(outputs * outputs, axis=-1, keepdims=True) + EPS)
                normed = outputs * inverse
                weighted = (normed * g[...] - t[0, 0, span, :].astype(jnp.float32)) * g[...]
                cross = jnp.mean(weighted * normed, axis=-1, keepdims=True)
                o[span, :] = (inverse * (weighted - normed * cross)).astype(o.dtype)

        def target_row(i, p):
            return (p[0] * 2 + p[2] if size == quarter else p[0]) * 2 + i

        block = pl.BlockSpec((tile, features), lambda i, p, c: (i, 0))
        return run(
            call(
                body,
                (2,),
                [
                    block,
                    block,
                    pl.BlockSpec((1, 1, tile, features), lambda i, p, c: (0, step, target_row(i, p), 0)),
                    pl.BlockSpec((1, features), lambda i, p, c: (0, 0)),
                ],
                block,
                jax.ShapeDtypeStruct((size, features), jnp.bfloat16),
                "norm_backward",
                8,
            ),
            place,
            summed,
            received,
            targets,
            gain,
        )

    def update(groups, grad_own, grad_other):
        total = len(groups)

        def body(p, c, *refs):
            go, gx = refs[:2]
            for i in range(total):
                ho, hx, w, o = (refs[2 + j * total + i] for j in range(4))
                grad = mm_rows(ho[0, 0], go[...]) + mm_rows(hx[0, 0], gx[...])
                grad = (FACTOR * grad).astype(jnp.bfloat16).astype(jnp.float32)
                o[...] = (w[0].astype(jnp.float32) - LEARN_RATE * grad).astype(o.dtype)

        def hidden_block(side, at, count):
            return pl.BlockSpec((1, 1, half, count * unit), lambda n, p, c: (0, 0, p[side], at // count))

        def weight_block(at, count):
            return pl.BlockSpec((1, count * unit, cols), lambda n, p, c: (0, at // count, n))

        return run(
            call(
                body,
                (4,),
                [grid_block((half, cols))] * 2
                + [hidden_block(0, *group) for group in groups]
                + [hidden_block(1, *group) for group in groups]
                + [weight_block(*group) for group in groups],
                [grid_block((count * unit, cols)) for _, count in groups],
                [jax.ShapeDtypeStruct((count * unit, features), jnp.bfloat16) for _, count in groups],
                "update",
                12,
            ),
            place,
            grad_own,
            grad_other,
            *[hidden] * (2 * total),
            *[weights] * total,
        )

    def begin(blocks):
        def body(p, c, h, *refs):
            *w, o = refs
            o[...] = sum(
                mm(h[0, 0, :, at * unit : (at + count) * unit], block[...])
                for (at, count), block in zip(GROUPS, w)
            )

        return run(
            call(
                body,
                (4,),
                [pl.BlockSpec((1, 1, tokens, ff), lambda n, p, c: (0, 1, 0, 0))]
                + [grid_block((count * unit, cols)) for _, count in GROUPS[:-1]],
                grid_block((tokens, cols)),
                jax.ShapeDtypeStruct((tokens, features), jnp.float32),
                "begin",
                20,
            ),
            place,
            hidden,
            *blocks,
        )

    def finish(begun, block):
        def body(p, c, a, h, w, *refs):
            *outs, acc = refs
            acc[...] = FACTOR * (a[...] + mm(h[0, 0], w[...]))
            for (left, right), o in zip(((1, 3), (1, 2), (0, 3), (0, 2)), outs):
                at = pl.multiple_of(p[left] * half + p[right] * quarter, quarter)
                o[...] = acc[pl.ds(at, quarter), :].astype(o.dtype)

        kinds = (jnp.bfloat16, jnp.bfloat16, jnp.float32, jnp.float32)
        return run(
            call(
                body,
                (4,),
                [
                    grid_block((tokens, cols)),
                    pl.BlockSpec((1, 1, tokens, 2 * unit), lambda n, p, c: (0, 1, 0, UNITS // 2 - 1)),
                    grid_block((2 * unit, cols)),
                ],
                [grid_block((quarter, cols))] * 4,
                [jax.ShapeDtypeStruct((quarter, features), kind) for kind in kinds],
                "finish",
                10,
                scratch=[pltpu.VMEM((tokens, cols), jnp.float32)],
            ),
            place,
            begun,
            hidden,
            block,
        )

    def gather_rows(p, scale, quarters, rows_of):
        spots = ((0, 2), (0, 3), (1, 2), (1, 3))
        for (left, right), q in zip(spots, quarters):
            at = pl.multiple_of(p[left] * half + p[right] * quarter, quarter)
            rows_of[pl.ds(at, quarter), :] = q[...] * scale

    def output_own(grads, own, got):
        def body(p, c, h, q0, q1, q2, q3, *refs):
            *refs, o, g = refs
            gather_rows(p, c[0].astype(jnp.bfloat16), (q0, q1, q2, q3), g)
            for i, (at, count) in enumerate(GROUPS):
                span = slice(at * unit, (at + count) * unit)
                base = c[0] * refs[i][...].astype(jnp.float32)
                if i < len(GROUPS) - 1:
                    base = base + c[1] * refs[len(GROUPS) + i][...].astype(jnp.float32)
                grad = mm_rows(h[0, 0, :, span], g[...])
                o[0, span, :] = (base - LEARN_RATE * FACTOR * grad).astype(o.dtype)

        blocks = [grid_block((count * unit, cols)) for _, count in GROUPS]
        return run(
            call(
                body,
                (4,),
                [pl.BlockSpec((1, 1, tokens, ff), lambda n, p, c: (0, 1, 0, 0))]
                + [grid_block((quarter, cols))] * 4
                + blocks
                + blocks[:-1],
                pl.BlockSpec((1, ff, cols), lambda n, p, c: (0, 0, n)),
                jax.ShapeDtypeStruct(weights.shape, weights.dtype),
                "output_own",
                28,
                scratch=[pltpu.VMEM((tokens, cols), jnp.bfloat16)],
            ),
            coef,
            hidden,
            *grads,
            *own,
            *got,
        )

    def output_far(grads, base, x_top, x_low):
        def body(p, c, ha, hb, q0, q1, q2, q3, b, xt, xl, o, g):
            gather_rows(p, c[1].astype(jnp.bfloat16), (q0, q1, q2, q3), g)
            for at, count in GROUPS:
                span = slice(at * unit, (at + count) * unit)
                first = at * unit - edge
                h = ha[:, span] if first < 0 else hb[:, first : first + count * unit]
                total = b[0, span, :].astype(jnp.float32) - LEARN_RATE * FACTOR * mm_rows(h, g[...])
                if at == UNITS - 2:
                    rest = jnp.concatenate([xt[...], xl[...]], axis=0)
                    total = total + c[1] * rest.astype(jnp.float32)
                o[0, span, :] = total.astype(o.dtype)

        whole = pl.BlockSpec((1, ff, narrow), lambda n, p, c: (0, 0, n))
        return run(
            call(
                body,
                (8,),
                [
                    pl.BlockSpec((tokens, edge), lambda n, p, c: (0, 0)),
                    pl.BlockSpec((tokens, ff - edge), lambda n, p, c: (0, 0)),
                ]
                + [grid_block((quarter, narrow))] * 4
                + [whole] + [grid_block((unit, narrow))] * 2,
                whole,
                jax.ShapeDtypeStruct(weights.shape, weights.dtype),
                "output_far",
                14,
                scratch=[pltpu.VMEM((tokens, narrow), jnp.bfloat16)],
            ),
            coef,
            *borrowed,
            *grads,
            base,
            x_top,
            x_low,
        )

    def mix(scale_a, a, scale_b, b):
        return (scale_a * a.astype(jnp.float32) + scale_b * b.astype(jnp.float32)).astype(jnp.bfloat16)

    def add(kept, *parts):
        return sum([part.astype(jnp.float32) for part in parts], kept).astype(jnp.bfloat16)

    sent, kept = forward()
    sent, raw_hidden, late = meet(sent, raw_hidden, stragglers)
    summed = add(kept, permute(sent, 0, 1))
    early_part, late_part = raw_hidden[0, 1, :, :edge], raw_hidden[0, 1, :, edge:]
    from_z = permute(summed, 0, 2)
    borrowed = [permute(early_part, 2, 0)]
    turn[0], borrowed[0] = meet(turn[0], borrowed[0])

    def pair(step, low, high):
        count = lax.dynamic_index_in_dim(late[step], low, keepdims=False)
        count += lax.dynamic_index_in_dim(late[step], high, keepdims=False)
        return jnp.where(count == 0, jnp.float32(0.5), jnp.float32(0.0))

    near, mine = pair(0, replica, replica ^ 1), pair(1, replica, replica ^ 2)
    coef = jnp.stack([1 - mine, mine])
    from_z, near, coef, late_part = meet(from_z, near, coef, late_part)
    borrowed.append(permute(late_part, 2, 0))

    grad_own = norm_backward(0, summed, from_z)
    grad_other = permute(grad_own, 0, 1)

    updated = update(GROUPS[:1], grad_own, grad_other)
    updated += update(GROUPS[1:], grad_own, grad_other)
    got = []
    for i in range(len(GROUPS)):
        if i > 1:
            updated[i], got[i - 2] = meet(updated[i], got[i - 2])
        got.append(permute(updated[i], 1, 0))
    averaged, x_got = [], []
    for i in range(len(GROUPS)):
        if i > 1:
            got[i], x_got[i - 2] = meet(got[i], x_got[i - 2])
        elif i == 0:
            got[i], borrowed[1] = meet(got[i], borrowed[1])
        if i == len(GROUPS) - 1:
            begun = begin(averaged)
            got[i], begun = meet(got[i], begun)
        averaged.append(mix(1 - near, updated[i], near, got[i]))
        if i < len(GROUPS) - 1:
            x_got.append(permute(averaged[i], 2, 0))

    sent_out, sent_stay, kept_out, kept_stay = finish(begun, averaged[-1])
    outgoing = add(kept_out, permute(sent_out, 0, 1))
    outgoing, x_got[-1] = meet(outgoing, x_got[-1])
    incoming = permute(outgoing, 0, 2)
    x_top = permute(averaged[-1][:unit], 2, 0)
    incoming, x_top = meet(incoming, x_top)
    staying = kept_stay + permute(sent_stay, 0, 1).astype(jnp.float32)
    mine_q = norm_backward(1, staying, incoming)
    final, mine_q = meet(averaged[-1][unit:], mine_q)
    near_q = permute(mine_q, 0, 2)
    far_q = permute(mine_q, 2, 0)
    near_q, far_q = meet(near_q, far_q)
    far_near = permute(far_q, 0, 2)
    x_low = permute(final, 2, 0)
    base = output_own((mine_q, near_q, permute(mine_q, 0, 1), permute(near_q, 0, 1)), averaged, x_got)
    far_near, base = meet(far_near, base)
    return output_far((far_q, far_near, permute(far_q, 0, 1), permute(far_near, 0, 1)), base, x_top, x_low)


def solution(mesh):
    placed = (
        P("replica", "tensor", None),
        P("replica", None, None, "tensor"),
        P("replica", None, None, None),
        P(),
        P(),
    )
    return jax.shard_map(
        on_device,
        mesh=mesh,
        in_specs=placed,
        out_specs=P("replica", "tensor", None),
        check_vma=False,
    )
```

```python
import jax
import jax.numpy as jnp
from jax import lax
from jax.experimental import pallas as pl
from jax.experimental.pallas import tpu as pltpu
from jax.sharding import PartitionSpec as P

FF = 7168
EPS = 1e-05
LEARN_RATE = 0.5
FACTOR = FF ** (-0.5)
UNITS = 14
GROUPS = tuple((2 * i, 2) for i in range(7))


def mm(left, right):
    return jnp.dot(left, right, preferred_element_type=jnp.float32)


def mm_rows(left, right):
    return lax.dot_general(left, right, (((0,), (0,)), ((), ())), preferred_element_type=jnp.float32)


def meet(*values):
    return lax.optimization_barrier(values)


def call(body, grid, in_specs, out_specs, out_shape, name, vmem_mib, aliases=None, scratch=()):
    return pl.pallas_call(
        body,
        grid_spec=pltpu.PrefetchScalarGridSpec(
            num_scalar_prefetch=2,
            grid=grid,
            in_specs=in_specs,
            out_specs=out_specs,
            scratch_shapes=list(scratch),
        ),
        out_shape=out_shape,
        input_output_aliases=aliases or {},
        compiler_params=pltpu.CompilerParams(vmem_limit_bytes=vmem_mib * 1024 * 1024),
        cost_estimate=pl.CostEstimate(flops=1, bytes_accessed=1, transcendentals=0),
        name=name,
    )


def on_device(weights, hidden, targets, norm_gain, stragglers):
    replicas, shards = lax.axis_size("replica"), lax.axis_size("tensor")
    tokens, ff = hidden.shape[2], hidden.shape[3]
    features = weights.shape[2]
    half = tokens // 2
    cols = features // 4
    unit = ff // UNITS
    deep = ff // 2
    edge = 6 * unit
    replica = lax.axis_index("replica")
    core = lax.rem(lax.axis_index("tensor"), 2)
    near_z = lax.div(lax.axis_index("tensor"), 2)
    quarter = tokens // 4
    gain = norm_gain.reshape(1, features)
    raw_hidden = hidden
    weights, hidden, targets = (pltpu.with_memory_space_constraint(a, pltpu.HBM) for a in (weights, hidden, targets))
    place = jnp.stack([core, 1 - core, near_z, 1 - near_z]).astype(jnp.int32)
    turn = [place]

    def permute(block, flip_replica, flip_tensor):
        route = [
            (r * shards + t, (r ^ flip_replica) * shards + (t ^ flip_tensor))
            for r in range(replicas)
            for t in range(shards)
        ]
        return lax.ppermute(block, ("replica", "tensor"), route)

    def run(kernel, *args):
        out = kernel(turn[0], *args)
        several = isinstance(out, (list, tuple))
        turn[0], *out = meet(turn[0], *(out if several else [out]))
        return out if several else out[0]

    def grid_block(shape):
        return pl.BlockSpec(shape, lambda n, p, c: (0, n))

    def forward():
        def body(p, c, h, w0, w1, send, keep, acc):
            total = mm(h[0, 0, :, :deep], w0[0]) + mm(h[0, 0, :, deep:], w1[0])
            acc[...] = FACTOR * total
            keep[...] = acc[pl.ds(pl.multiple_of(p[0] * half, half), half), :]
            send[...] = acc[pl.ds(pl.multiple_of(p[1] * half, half), half), :].astype(send.dtype)

        return run(
            call(
                body,
                (4,),
                [
                    pl.BlockSpec((1, 1, tokens, ff), lambda n, p, c: (0, 0, 0, 0)),
                    pl.BlockSpec((1, deep, cols), lambda n, p, c: (0, 0, n)),
                    pl.BlockSpec((1, deep, cols), lambda n, p, c: (0, 1, n)),
                ],
                [grid_block((half, cols))] * 2,
                [
                    jax.ShapeDtypeStruct((half, features), jnp.bfloat16),
                    jax.ShapeDtypeStruct((half, features), jnp.float32),
                ],
                "forward",
                14,
                scratch=[pltpu.VMEM((tokens, cols), jnp.float32)],
            ),
            place,
            hidden,
            weights,
            weights,
        )

    def norm_backward(step, summed, received):
        size = summed.shape[0]
        tile = size // 2
        strip = min(16, tile)

        def body(p, c, s, r, t, g, o):
            for i in range(tile // strip):
                span = slice(i * strip, (i + 1) * strip)
                outputs = s[span, :].astype(jnp.float32) + r[span, :].astype(jnp.float32)
                inverse = lax.rsqrt(jnp.mean(outputs * outputs, axis=-1, keepdims=True) + EPS)
                normed = outputs * inverse
                weighted = (normed * g[...] - t[0, 0, span, :].astype(jnp.float32)) * g[...]
                cross = jnp.mean(weighted * normed, axis=-1, keepdims=True)
                o[span, :] = (inverse * (weighted - normed * cross)).astype(o.dtype)

        def target_row(i, p):
            return (p[0] * 2 + p[2] if size == quarter else p[0]) * 2 + i

        block = pl.BlockSpec((tile, features), lambda i, p, c: (i, 0))
        return run(
            call(
                body,
                (2,),
                [
                    block,
                    block,
                    pl.BlockSpec((1, 1, tile, features), lambda i, p, c: (0, step, target_row(i, p), 0)),
                    pl.BlockSpec((1, features), lambda i, p, c: (0, 0)),
                ],
                block,
                jax.ShapeDtypeStruct((size, features), jnp.bfloat16),
                "norm_backward",
                8,
            ),
            place,
            summed,
            received,
            targets,
            gain,
        )

    def update(groups, grad_own, grad_other):
        total = len(groups)
        across = cols if total > 1 else 2 * cols

        def body(p, c, *refs):
            go, gx = refs[:2]
            for i in range(total):
                ho, hx, w, o = (refs[2 + j * total + i] for j in range(4))
                grad = mm_rows(ho[0, 0], go[...]) + mm_rows(hx[0, 0], gx[...])
                grad = (FACTOR * grad).astype(jnp.bfloat16).astype(jnp.float32)
                o[...] = (w[0].astype(jnp.float32) - LEARN_RATE * grad).astype(o.dtype)

        def hidden_block(side, at, count):
            return pl.BlockSpec((1, 1, half, count * unit), lambda n, p, c: (0, 0, p[side], at // count))

        def weight_block(at, count):
            return pl.BlockSpec((1, count * unit, across), lambda n, p, c: (0, at // count, n))

        return run(
            call(
                body,
                (features // across,),
                [grid_block((half, across))] * 2
                + [hidden_block(0, *group) for group in groups]
                + [hidden_block(1, *group) for group in groups]
                + [weight_block(*group) for group in groups],
                [grid_block((count * unit, across)) for _, count in groups],
                [jax.ShapeDtypeStruct((count * unit, features), jnp.bfloat16) for _, count in groups],
                "update",
                12,
            ),
            place,
            grad_own,
            grad_other,
            *[hidden] * (2 * total),
            *[weights] * total,
        )

    def begin(blocks):
        def body(p, c, h, *refs):
            *w, o = refs
            o[...] = sum(
                mm(h[0, 0, :, at * unit : (at + count) * unit], block[...])
                for (at, count), block in zip(GROUPS, w)
            )

        return run(
            call(
                body,
                (4,),
                [pl.BlockSpec((1, 1, tokens, ff), lambda n, p, c: (0, 1, 0, 0))]
                + [grid_block((count * unit, cols)) for _, count in GROUPS[:-1]],
                grid_block((tokens, cols)),
                jax.ShapeDtypeStruct((tokens, features), jnp.float32),
                "begin",
                20,
            ),
            place,
            hidden,
            *blocks,
        )

    def finish(begun, block):
        def body(p, c, a, h, w, *refs):
            *outs, acc = refs
            acc[...] = FACTOR * (a[...] + mm(h[0, 0], w[...]))
            for (left, right), o in zip(((1, 3), (1, 2), (0, 3), (0, 2)), outs):
                at = pl.multiple_of(p[left] * half + p[right] * quarter, quarter)
                o[...] = acc[pl.ds(at, quarter), :].astype(o.dtype)

        kinds = (jnp.bfloat16, jnp.bfloat16, jnp.float32, jnp.float32)
        return run(
            call(
                body,
                (4,),
                [
                    grid_block((tokens, cols)),
                    pl.BlockSpec((1, 1, tokens, 2 * unit), lambda n, p, c: (0, 1, 0, UNITS // 2 - 1)),
                    grid_block((2 * unit, cols)),
                ],
                [grid_block((quarter, cols))] * 4,
                [jax.ShapeDtypeStruct((quarter, features), kind) for kind in kinds],
                "finish",
                10,
                scratch=[pltpu.VMEM((tokens, cols), jnp.float32)],
            ),
            place,
            begun,
            hidden,
            block,
        )

    def gather_rows(p, scale, quarters, rows_of):
        spots = ((0, 2), (0, 3), (1, 2), (1, 3))
        for (left, right), q in zip(spots, quarters):
            at = pl.multiple_of(p[left] * half + p[right] * quarter, quarter)
            rows_of[pl.ds(at, quarter), :] = q[...] * scale

    def output_own(grads, own, got):
        def body(p, c, h, q0, q1, q2, q3, *refs):
            *refs, o, g = refs
            gather_rows(p, c[0].astype(jnp.bfloat16), (q0, q1, q2, q3), g)
            for i, (at, count) in enumerate(GROUPS):
                span = slice(at * unit, (at + count) * unit)
                base = c[0] * refs[i][...].astype(jnp.float32)
                if i < len(GROUPS) - 1:
                    base = base + c[1] * refs[len(GROUPS) + i][...].astype(jnp.float32)
                grad = mm_rows(h[0, 0, :, span], g[...])
                o[0, span, :] = (base - LEARN_RATE * FACTOR * grad).astype(o.dtype)

        blocks = [grid_block((count * unit, cols)) for _, count in GROUPS]
        return run(
            call(
                body,
                (4,),
                [pl.BlockSpec((1, 1, tokens, ff), lambda n, p, c: (0, 1, 0, 0))]
                + [grid_block((quarter, cols))] * 4
                + blocks
                + blocks[:-1],
                pl.BlockSpec((1, ff, cols), lambda n, p, c: (0, 0, n)),
                jax.ShapeDtypeStruct(weights.shape, weights.dtype),
                "output_own",
                28,
                scratch=[pltpu.VMEM((tokens, cols), jnp.bfloat16)],
            ),
            coef,
            hidden,
            *grads,
            *own,
            *got,
        )

    def output_far(grads, base, x_top, x_low):
        tall = 2 * unit
        early = edge // tall
        last = UNITS // 2 - 1

        def body(p, c, ha, hb, q0, q1, q2, q3, b, xt, xl, o, g):
            step = pl.program_id(0)

            @pl.when(step == 0)
            def _():
                gather_rows(p, c[1].astype(jnp.bfloat16), (q0, q1, q2, q3), g)

            def emit(h, extra):
                for j in range(4):
                    side = slice(j * cols, (j + 1) * cols)
                    total = b[0, :, side].astype(jnp.float32)
                    total = total - LEARN_RATE * FACTOR * mm_rows(h[...], g[:, side])
                    if extra:
                        rest = jnp.concatenate([xt[:, side], xl[:, side]], axis=0)
                        total = total + c[1] * rest.astype(jnp.float32)
                    o[0, :, side] = total.astype(o.dtype)

            pl.when(step < early)(lambda: emit(ha, False))
            pl.when((step >= early) & (step < last))(lambda: emit(hb, False))
            pl.when(step == last)(lambda: emit(hb, True))

        def fixed(height):
            return pl.BlockSpec((height, features), lambda n, p, c: (0, 0))

        block = pl.BlockSpec((1, tall, features), lambda n, p, c: (0, n, 0))
        return run(
            call(
                body,
                (UNITS // 2,),
                [
                    pl.BlockSpec((tokens, tall), lambda n, p, c: (0, jnp.minimum(n, early - 1))),
                    pl.BlockSpec((tokens, tall), lambda n, p, c: (0, jnp.maximum(n - early, 0))),
                ]
                + [fixed(quarter)] * 4
                + [block, fixed(unit), fixed(unit)],
                block,
                jax.ShapeDtypeStruct(weights.shape, weights.dtype),
                "output_far",
                18,
                scratch=[pltpu.VMEM((tokens, features), jnp.bfloat16)],
            ),
            coef,
            *borrowed,
            *grads,
            base,
            x_top,
            x_low,
        )

    def mix(scale_a, a, scale_b, b):
        return (scale_a * a.astype(jnp.float32) + scale_b * b.astype(jnp.float32)).astype(jnp.bfloat16)

    def add(kept, *parts):
        return sum([part.astype(jnp.float32) for part in parts], kept).astype(jnp.bfloat16)

    sent, kept = forward()
    summed = add(kept, permute(sent, 0, 1))
    summed, raw_hidden, late = meet(summed, raw_hidden, stragglers)
    early_part, late_part = raw_hidden[0, 1, :, :edge], raw_hidden[0, 1, :, edge:]
    from_z = permute(summed, 0, 2)
    borrowed = [permute(early_part, 2, 0)]
    turn[0], borrowed[0] = meet(turn[0], borrowed[0])

    def pair(step, low, high):
        count = lax.dynamic_index_in_dim(late[step], low, keepdims=False)
        count += lax.dynamic_index_in_dim(late[step], high, keepdims=False)
        return jnp.where(count == 0, jnp.float32(0.5), jnp.float32(0.0))

    near, mine = pair(0, replica, replica ^ 1), pair(1, replica, replica ^ 2)
    coef = jnp.stack([1 - mine, mine])
    from_z, near, coef, late_part = meet(from_z, near, coef, late_part)
    borrowed.append(permute(late_part, 2, 0))

    grad_own = norm_backward(0, summed, from_z)
    grad_other = permute(grad_own, 0, 1)

    updated = update(GROUPS[:1], grad_own, grad_other)
    updated += update(GROUPS[1:], grad_own, grad_other)
    got = []
    for i in range(len(GROUPS)):
        if i > 1:
            updated[i], got[i - 2] = meet(updated[i], got[i - 2])
        got.append(permute(updated[i], 1, 0))
    averaged, x_got = [], []
    for i in range(len(GROUPS)):
        if i > 1:
            got[i], x_got[i - 2] = meet(got[i], x_got[i - 2])
        elif i == 0:
            got[i], borrowed[1] = meet(got[i], borrowed[1])
        if i == len(GROUPS) - 1:
            begun = begin(averaged)
            got[i], begun = meet(got[i], begun)
        averaged.append(mix(1 - near, updated[i], near, got[i]))
        if i < len(GROUPS) - 1:
            x_got.append(permute(averaged[i], 2, 0))

    sent_out, sent_stay, kept_out, kept_stay = finish(begun, averaged[-1])
    outgoing = add(kept_out, permute(sent_out, 0, 1))
    outgoing, x_got[-1] = meet(outgoing, x_got[-1])
    incoming = permute(outgoing, 0, 2)
    x_top = permute(averaged[-1][:unit], 2, 0)
    incoming, x_top = meet(incoming, x_top)
    staying = kept_stay + permute(sent_stay, 0, 1).astype(jnp.float32)
    mine_q = norm_backward(1, staying, incoming)
    final, mine_q = meet(averaged[-1][unit:], mine_q)
    near_q = permute(mine_q, 0, 2)
    far_q = permute(mine_q, 2, 0)
    near_q, far_q = meet(near_q, far_q)
    far_near = permute(far_q, 0, 2)
    x_low = permute(final, 2, 0)
    base = output_own((mine_q, near_q, permute(mine_q, 0, 1), permute(near_q, 0, 1)), averaged, x_got)
    far_near, base = meet(far_near, base)
    return output_far((far_q, far_near, permute(far_q, 0, 1), permute(far_near, 0, 1)), base, x_top, x_low)


def solution(mesh):
    placed = (
        P("replica", "tensor", None),
        P("replica", None, None, "tensor"),
        P("replica", None, None, None),
        P(),
        P(),
    )
    return jax.shard_map(
        on_device,
        mesh=mesh,
        in_specs=placed,
        out_specs=P("replica", "tensor", None),
        check_vma=False,
    )
```

```python
import jax
import jax.numpy as jnp
from jax import lax
from jax.experimental import pallas as pl
from jax.experimental.pallas import tpu as pltpu
from jax.sharding import PartitionSpec as P

FF = 7168
EPS = 1e-05
LEARN_RATE = 0.5
FACTOR = FF ** (-0.5)
UNITS = 14
GROUPS = tuple((2 * i, 2) for i in range(7))


def mm(left, right):
    return jnp.dot(left, right, preferred_element_type=jnp.float32)


def mm_rows(left, right):
    return lax.dot_general(left, right, (((0,), (0,)), ((), ())), preferred_element_type=jnp.float32)


def meet(*values):
    return lax.optimization_barrier(values)


def call(body, grid, in_specs, out_specs, out_shape, name, vmem_mib, aliases=None, scratch=()):
    return pl.pallas_call(
        body,
        grid_spec=pltpu.PrefetchScalarGridSpec(
            num_scalar_prefetch=2,
            grid=grid,
            in_specs=in_specs,
            out_specs=out_specs,
            scratch_shapes=list(scratch),
        ),
        out_shape=out_shape,
        input_output_aliases=aliases or {},
        compiler_params=pltpu.CompilerParams(vmem_limit_bytes=vmem_mib * 1024 * 1024),
        cost_estimate=pl.CostEstimate(flops=1, bytes_accessed=1, transcendentals=0),
        name=name,
    )


def on_device(weights, hidden, targets, norm_gain, stragglers):
    replicas, shards = lax.axis_size("replica"), lax.axis_size("tensor")
    tokens, ff = hidden.shape[2], hidden.shape[3]
    features = weights.shape[2]
    half = tokens // 2
    cols = features // 4
    unit = ff // UNITS
    deep = ff // 2
    edge = 6 * unit
    replica = lax.axis_index("replica")
    core = lax.rem(lax.axis_index("tensor"), 2)
    near_z = lax.div(lax.axis_index("tensor"), 2)
    quarter = tokens // 4
    gain = norm_gain.reshape(1, features)
    raw_hidden = hidden
    weights, hidden, targets = (pltpu.with_memory_space_constraint(a, pltpu.HBM) for a in (weights, hidden, targets))
    place = jnp.stack([core, 1 - core, near_z, 1 - near_z]).astype(jnp.int32)
    turn = [place]

    def permute(block, flip_replica, flip_tensor):
        route = [
            (r * shards + t, (r ^ flip_replica) * shards + (t ^ flip_tensor))
            for r in range(replicas)
            for t in range(shards)
        ]
        return lax.ppermute(block, ("replica", "tensor"), route)

    def run(kernel, *args):
        out = kernel(turn[0], *args)
        several = isinstance(out, (list, tuple))
        turn[0], *out = meet(turn[0], *(out if several else [out]))
        return out if several else out[0]

    def grid_block(shape):
        return pl.BlockSpec(shape, lambda n, p, c: (0, n))

    def forward():
        def body(p, c, h, w0, w1, send, keep, acc):
            total = mm(h[0, 0, :, :deep], w0[0]) + mm(h[0, 0, :, deep:], w1[0])
            acc[...] = FACTOR * total
            keep[...] = acc[pl.ds(pl.multiple_of(p[0] * half, half), half), :]
            send[...] = acc[pl.ds(pl.multiple_of(p[1] * half, half), half), :].astype(send.dtype)

        return run(
            call(
                body,
                (4,),
                [
                    pl.BlockSpec((1, 1, tokens, ff), lambda n, p, c: (0, 0, 0, 0)),
                    pl.BlockSpec((1, deep, cols), lambda n, p, c: (0, 0, n)),
                    pl.BlockSpec((1, deep, cols), lambda n, p, c: (0, 1, n)),
                ],
                [grid_block((half, cols))] * 2,
                [
                    jax.ShapeDtypeStruct((half, features), jnp.bfloat16),
                    jax.ShapeDtypeStruct((half, features), jnp.float32),
                ],
                "forward",
                14,
                scratch=[pltpu.VMEM((tokens, cols), jnp.float32)],
            ),
            place,
            hidden,
            weights,
            weights,
        )

    def norm_backward(step, summed, received):
        size = summed.shape[0]
        tile = size // 2
        strip = min(16, tile)

        def body(p, c, s, r, t, g, o):
            for i in range(tile // strip):
                span = slice(i * strip, (i + 1) * strip)
                outputs = s[span, :].astype(jnp.float32) + r[span, :].astype(jnp.float32)
                inverse = lax.rsqrt(jnp.mean(outputs * outputs, axis=-1, keepdims=True) + EPS)
                normed = outputs * inverse
                weighted = (normed * g[...] - t[0, 0, span, :].astype(jnp.float32)) * g[...]
                cross = jnp.mean(weighted * normed, axis=-1, keepdims=True)
                o[span, :] = (inverse * (weighted - normed * cross)).astype(o.dtype)

        def target_row(i, p):
            return (p[0] * 2 + p[2] if size == quarter else p[0]) * 2 + i

        block = pl.BlockSpec((tile, features), lambda i, p, c: (i, 0))
        return run(
            call(
                body,
                (2,),
                [
                    block,
                    block,
                    pl.BlockSpec((1, 1, tile, features), lambda i, p, c: (0, step, target_row(i, p), 0)),
                    pl.BlockSpec((1, features), lambda i, p, c: (0, 0)),
                ],
                block,
                jax.ShapeDtypeStruct((size, features), jnp.bfloat16),
                "norm_backward",
                8,
            ),
            place,
            summed,
            received,
            targets,
            gain,
        )

    def update(groups, grad_own, grad_other):
        total = len(groups)
        across = cols if total > 1 else 2 * cols

        def body(p, c, *refs):
            go, gx = refs[:2]
            for i in range(total):
                ho, hx, w, o = (refs[2 + j * total + i] for j in range(4))
                grad = mm_rows(ho[0, 0], go[...]) + mm_rows(hx[0, 0], gx[...])
                grad = (FACTOR * grad).astype(jnp.bfloat16).astype(jnp.float32)
                o[...] = (w[0].astype(jnp.float32) - LEARN_RATE * grad).astype(o.dtype)

        def hidden_block(side, at, count):
            return pl.BlockSpec((1, 1, half, count * unit), lambda n, p, c: (0, 0, p[side], at // count))

        def weight_block(at, count):
            return pl.BlockSpec((1, count * unit, across), lambda n, p, c: (0, at // count, n))

        return run(
            call(
                body,
                (features // across,),
                [grid_block((half, across))] * 2
                + [hidden_block(0, *group) for group in groups]
                + [hidden_block(1, *group) for group in groups]
                + [weight_block(*group) for group in groups],
                [grid_block((count * unit, across)) for _, count in groups],
                [jax.ShapeDtypeStruct((count * unit, features), jnp.bfloat16) for _, count in groups],
                "update",
                12,
            ),
            place,
            grad_own,
            grad_other,
            *[hidden] * (2 * total),
            *[weights] * total,
        )

    def begin(blocks):
        def body(p, c, h, *refs):
            *w, o = refs
            o[...] = sum(
                mm(h[0, 0, :, at * unit : (at + count) * unit], block[...])
                for (at, count), block in zip(GROUPS, w)
            )

        return run(
            call(
                body,
                (4,),
                [pl.BlockSpec((1, 1, tokens, ff), lambda n, p, c: (0, 1, 0, 0))]
                + [grid_block((count * unit, cols)) for _, count in GROUPS[:-1]],
                grid_block((tokens, cols)),
                jax.ShapeDtypeStruct((tokens, features), jnp.float32),
                "begin",
                20,
            ),
            place,
            hidden,
            *blocks,
        )

    def finish(begun, block):
        def body(p, c, a, h, w, *refs):
            *outs, acc = refs
            acc[...] = FACTOR * (a[...] + mm(h[0, 0], w[...]))
            for (left, right), o in zip(((1, 3), (1, 2), (0, 3), (0, 2)), outs):
                at = pl.multiple_of(p[left] * half + p[right] * quarter, quarter)
                o[...] = acc[pl.ds(at, quarter), :].astype(o.dtype)

        kinds = (jnp.bfloat16, jnp.bfloat16, jnp.float32, jnp.float32)
        return run(
            call(
                body,
                (2,),
                [
                    grid_block((tokens, 2 * cols)),
                    pl.BlockSpec((1, 1, tokens, 2 * unit), lambda n, p, c: (0, 1, 0, UNITS // 2 - 1)),
                    grid_block((2 * unit, 2 * cols)),
                ],
                [grid_block((quarter, 2 * cols))] * 4,
                [jax.ShapeDtypeStruct((quarter, features), kind) for kind in kinds],
                "finish",
                20,
                scratch=[pltpu.VMEM((tokens, 2 * cols), jnp.float32)],
            ),
            place,
            begun,
            hidden,
            block,
        )

    def gather_rows(p, scale, quarters, rows_of):
        spots = ((0, 2), (0, 3), (1, 2), (1, 3))
        for (left, right), q in zip(spots, quarters):
            at = pl.multiple_of(p[left] * half + p[right] * quarter, quarter)
            rows_of[pl.ds(at, quarter), :] = q[...] * scale

    def output_own(grads, own, got):
        def body(p, c, h, q0, q1, q2, q3, *refs):
            *refs, o, g = refs
            gather_rows(p, c[0].astype(jnp.bfloat16), (q0, q1, q2, q3), g)
            for i, (at, count) in enumerate(GROUPS):
                span = slice(at * unit, (at + count) * unit)
                base = c[0] * refs[i][...].astype(jnp.float32)
                if i < len(GROUPS) - 1:
                    base = base + c[1] * refs[len(GROUPS) + i][...].astype(jnp.float32)
                grad = mm_rows(h[0, 0, :, span], g[...])
                o[0, span, :] = (base - LEARN_RATE * FACTOR * grad).astype(o.dtype)

        blocks = [grid_block((count * unit, cols)) for _, count in GROUPS]
        return run(
            call(
                body,
                (4,),
                [pl.BlockSpec((1, 1, tokens, ff), lambda n, p, c: (0, 1, 0, 0))]
                + [grid_block((quarter, cols))] * 4
                + blocks
                + blocks[:-1],
                pl.BlockSpec((1, ff, cols), lambda n, p, c: (0, 0, n)),
                jax.ShapeDtypeStruct(weights.shape, weights.dtype),
                "output_own",
                28,
                scratch=[pltpu.VMEM((tokens, cols), jnp.bfloat16)],
            ),
            coef,
            hidden,
            *grads,
            *own,
            *got,
        )

    def output_far(grads, base, x_top, x_low):
        tall = 2 * unit
        early = edge // tall
        last = UNITS // 2 - 1

        def body(p, c, ha, hb, q0, q1, q2, q3, b, xt, xl, o, g):
            step = pl.program_id(0)

            @pl.when(step == 0)
            def _():
                gather_rows(p, c[1].astype(jnp.bfloat16), (q0, q1, q2, q3), g)

            def emit(h, extra):
                for j in range(4):
                    side = slice(j * cols, (j + 1) * cols)
                    total = b[0, :, side].astype(jnp.float32)
                    total = total - LEARN_RATE * FACTOR * mm_rows(h[...], g[:, side])
                    if extra:
                        rest = jnp.concatenate([xt[:, side], xl[:, side]], axis=0)
                        total = total + c[1] * rest.astype(jnp.float32)
                    o[0, :, side] = total.astype(o.dtype)

            pl.when(step < early)(lambda: emit(ha, False))
            pl.when((step >= early) & (step < last))(lambda: emit(hb, False))
            pl.when(step == last)(lambda: emit(hb, True))

        def fixed(height):
            return pl.BlockSpec((height, features), lambda n, p, c: (0, 0))

        block = pl.BlockSpec((1, tall, features), lambda n, p, c: (0, n, 0))
        return run(
            call(
                body,
                (UNITS // 2,),
                [
                    pl.BlockSpec((tokens, tall), lambda n, p, c: (0, jnp.minimum(n, early - 1))),
                    pl.BlockSpec((tokens, tall), lambda n, p, c: (0, jnp.maximum(n - early, 0))),
                ]
                + [fixed(quarter)] * 4
                + [block, fixed(unit), fixed(unit)],
                block,
                jax.ShapeDtypeStruct(weights.shape, weights.dtype),
                "output_far",
                18,
                scratch=[pltpu.VMEM((tokens, features), jnp.bfloat16)],
            ),
            coef,
            *borrowed,
            *grads,
            base,
            x_top,
            x_low,
        )

    def mix(scale_a, a, scale_b, b):
        return (scale_a * a.astype(jnp.float32) + scale_b * b.astype(jnp.float32)).astype(jnp.bfloat16)

    def add(kept, *parts):
        return sum([part.astype(jnp.float32) for part in parts], kept).astype(jnp.bfloat16)

    sent, kept = forward()
    summed = add(kept, permute(sent, 0, 1))
    summed, raw_hidden, late = meet(summed, raw_hidden, stragglers)
    early_part, late_part = raw_hidden[0, 1, :, :edge], raw_hidden[0, 1, :, edge:]
    from_z = permute(summed, 0, 2)
    borrowed = [permute(early_part, 2, 0)]
    turn[0], borrowed[0] = meet(turn[0], borrowed[0])

    def pair(step, low, high):
        count = lax.dynamic_index_in_dim(late[step], low, keepdims=False)
        count += lax.dynamic_index_in_dim(late[step], high, keepdims=False)
        return jnp.where(count == 0, jnp.float32(0.5), jnp.float32(0.0))

    near, mine = pair(0, replica, replica ^ 1), pair(1, replica, replica ^ 2)
    coef = jnp.stack([1 - mine, mine])
    from_z, near, coef, late_part = meet(from_z, near, coef, late_part)
    borrowed.append(permute(late_part, 2, 0))

    grad_own = norm_backward(0, summed, from_z)
    grad_other = permute(grad_own, 0, 1)

    updated = update(GROUPS[:1], grad_own, grad_other)
    updated += update(GROUPS[1:], grad_own, grad_other)
    got = []
    for i in range(len(GROUPS)):
        if i > 1:
            updated[i], got[i - 2] = meet(updated[i], got[i - 2])
        got.append(permute(updated[i], 1, 0))
    averaged, x_got = [], []
    for i in range(len(GROUPS)):
        if i > 1:
            got[i], x_got[i - 2] = meet(got[i], x_got[i - 2])
        elif i == 0:
            got[i], borrowed[1] = meet(got[i], borrowed[1])
        if i == len(GROUPS) - 1:
            begun = begin(averaged)
            got[i], begun = meet(got[i], begun)
        averaged.append(mix(1 - near, updated[i], near, got[i]))
        if i < len(GROUPS) - 1:
            x_got.append(permute(averaged[i], 2, 0))

    sent_out, sent_stay, kept_out, kept_stay = finish(begun, averaged[-1])
    outgoing = add(kept_out, permute(sent_out, 0, 1))
    outgoing, top, x_got[-1] = meet(outgoing, averaged[-1][:unit], x_got[-1])
    incoming = permute(outgoing, 0, 2)
    x_top = permute(top, 2, 0)
    staying = kept_stay + permute(sent_stay, 0, 1).astype(jnp.float32)
    mine_q = norm_backward(1, staying, incoming)
    final, mine_q = meet(averaged[-1][unit:], mine_q)
    near_q = permute(mine_q, 0, 2)
    far_q = permute(mine_q, 2, 0)
    near_q, far_q, x_top = meet(near_q, far_q, x_top)
    far_near = permute(far_q, 0, 2)
    x_low = permute(final, 2, 0)
    base = output_own((mine_q, near_q, permute(mine_q, 0, 1), permute(near_q, 0, 1)), averaged, x_got)
    far_near, base = meet(far_near, base)
    return output_far((far_q, far_near, permute(far_q, 0, 1), permute(far_near, 0, 1)), base, x_top, x_low)


def solution(mesh):
    placed = (
        P("replica", "tensor", None),
        P("replica", None, None, "tensor"),
        P("replica", None, None, None),
        P(),
        P(),
    )
    return jax.shard_map(
        on_device,
        mesh=mesh,
        in_specs=placed,
        out_specs=P("replica", "tensor", None),
        check_vma=False,
    )
```
